32 devices in a mesh: groups: 2 (over y), seq: 16 (over z, x, core).
Axes of the slice: x: 2, y: 2, z: 4, core: 2. Of those that a mesh axis runs over, the one named last changes fastest.
Arguments:
- queries: bfloat16 [4096, 3072], P(('groups', 'seq')), parts along dimension 0, may hold values from -8 to 8
- keys: bfloat16 [4096, 3072], P(('groups', 'seq')), parts along dimension 0, may hold values from -6 to 6
- values: bfloat16 [4096, 3072], P(('groups', 'seq')), parts along dimension 0, may hold values from -6 to 6
- rand_blocks: int32 [32, 3], P('groups'), parts along dimension 0, may hold values from 0 to 15, as said below
- global_ids: int32 [4], P('groups'), parts along dimension 0, may hold values from 0 to 15, as said below
Outputs:
- attended: bfloat16 [4096, 3072], P(('groups', 'seq')), parts along dimension 0
The draws below stay inside these ranges and needn't reach their ends.
There are 2 independent parts, one for each index of `groups`. The reference program is written for one: setup_inputs(seed, part) draws one part's arguments, and reference() takes and returns one part's arrays. A program takes and returns all parts, laid end to end along the dimension named above; each array names one. Nothing has to cross between parts.
Inputs may be any that keep to these rules, and one draw needn't show every extreme that they name: `rand_blocks`: row b names 3 different blocks, none of them b-1, b, b+1 or a global block. `global_ids`: 2 different blocks, one of which is the last block.
All inputs are finite; a program needn't handle non-finite values.
Results may differ from the reference program's by a relative error of at most 0.0049.
Values may be sent and summed in bfloat16 or wider, within the bound.
A program may use at most 128 MiB of HBM per device.

```python
import jax
import jax.numpy as jnp
from jax import lax

HEADS = 24
HEAD_DIM = 128
BLOCK = 128
GLOBALS = 2
RANDOMS = 3
WIDTH = 3072
NBLOCKS = 16
TOKENS = 2048


def query_key_pair(key):
    base_queries = jax.random.normal(jax.random.fold_in(key, 101), (TOKENS, WIDTH), jnp.float32)
    base_keys = jax.random.normal(jax.random.fold_in(key, 102), (TOKENS, WIDTH), jnp.float32)
    drawn_queries = 2.2 * jnp.clip(base_queries, -2.7, 2.7)
    drawn_keys = jnp.clip(base_keys, -4.0, 4.0)
    return (drawn_queries, drawn_keys)


def draw_queries(key, part):
    return query_key_pair(key)[0].astype(jnp.bfloat16)


def draw_keys(key, part):
    return query_key_pair(key)[1].astype(jnp.bfloat16)


def block_tables(key):
    others = jax.random.permutation(jax.random.fold_in(key, 201), NBLOCKS - 1)[:GLOBALS - 1].astype(jnp.int32)
    chosen_globals = jnp.concatenate([others, jnp.full((1,), NBLOCKS - 1, dtype=jnp.int32)]).astype(jnp.int32)
    columns = jnp.arange(NBLOCKS, dtype=jnp.int32)
    rows = columns[:, None]
    scores = jax.random.randint(jax.random.fold_in(key, 202), (NBLOCKS, NBLOCKS), 0, 2 ** 20, dtype=jnp.int32) * NBLOCKS + columns[None, :]
    near = jnp.abs(columns[None, :] - rows) <= 1
    global_column = jnp.any(columns[:, None] == chosen_globals[None, :], axis=1)[None, :]
    scores = jnp.where(near | global_column, -1, scores)
    picked = lax.top_k(scores, RANDOMS)[1].astype(jnp.int32)
    return (picked, chosen_globals)


def draw_rand_blocks(key, part):
    return block_tables(key)[0]


def draw_global_ids(key, part):
    return block_tables(key)[1]


def level_of(own_key, extent, split, low, largest):
    loudness, own = 1.0, jax.random.fold_in(own_key, 6)
    for axis_at, parts in split:
        draws = jnp.exp(jax.random.uniform(jax.random.fold_in(own, axis_at), (parts,), jnp.float32, low / len(split), largest / len(split)))
        loudness = loudness * jnp.repeat(draws, extent[axis_at] // parts).reshape([-1 if axis == axis_at else 1 for axis in range(len(extent))])
    return loudness


def normal_values(stream_key, shape, width, bound, split=(), kind=jnp.bfloat16):
    values = jax.random.normal(stream_key, shape, jnp.float32) * width
    if len(split) > 0:
        values = level_of(stream_key, shape, split, -0.22, 0.18) * values
    return jnp.clip(values, min=-bound, max=bound).astype(kind)


def setup_inputs(seed: int = 0, part: int = 0) -> dict:
    key_of = jax.random.split(jax.random.key(seed), 6)
    own_keys = jax.random.split(jax.random.fold_in(key_of[5], part), 6)
    return {
        "queries": draw_queries(jax.random.fold_in(jax.random.fold_in(key_of[5], part), 71), part),
        "keys": draw_keys(jax.random.fold_in(jax.random.fold_in(key_of[5], part), 71), part),
        "values": normal_values(own_keys[2], (TOKENS, WIDTH), 1.0, 6.0, ((0, 16),)),
        "rand_blocks": draw_rand_blocks(jax.random.fold_in(jax.random.fold_in(key_of[5], part), 71), part),
        "global_ids": draw_global_ids(jax.random.fold_in(jax.random.fold_in(key_of[5], part), 71), part),
    }


def reference(queries, keys, values, rand_blocks, global_ids):
    query_blocks = queries.reshape(NBLOCKS, BLOCK, HEADS, HEAD_DIM)
    key_blocks = keys.reshape(NBLOCKS, BLOCK, HEADS, HEAD_DIM)
    value_blocks = values.reshape(NBLOCKS, BLOCK, HEADS, HEAD_DIM)
    scale = HEAD_DIM ** -0.5

    def one_block(block_id):
        window = block_id + jnp.arange(-1, 2, dtype=jnp.int32)
        global_hit = jnp.any(window[:, None] == global_ids[None, :], axis=1)
        window_ok = (window >= 0) & (window < NBLOCKS) & jnp.logical_not(global_hit)
        wanted = jnp.concatenate([window, global_ids.astype(jnp.int32), rand_blocks[block_id].astype(jnp.int32)])
        usable = jnp.concatenate([window_ok, jnp.ones((GLOBALS + RANDOMS,), dtype=bool)])
        index = jnp.clip(wanted, 0, NBLOCKS - 1).astype(jnp.int32)
        chosen_keys = key_blocks[index].astype(jnp.float32)
        chosen_values = value_blocks[index].astype(jnp.float32)
        own_queries = query_blocks[block_id].astype(jnp.float32)
        scores = jnp.einsum('qhd,jkhd->hqjk', own_queries, chosen_keys) * scale
        scores = jnp.where(usable[None, None, :, None], scores, -1e30)
        top = jnp.max(scores, axis=(2, 3), keepdims=True)
        powers = jnp.exp(scores - top)
        total = jnp.sum(powers, axis=(2, 3), keepdims=True)
        probs = (powers / total).astype(jnp.bfloat16)
        result = jnp.einsum('hqjk,jkhd->qhd', probs.astype(jnp.float32), chosen_values)
        return result.reshape(BLOCK, WIDTH).astype(jnp.bfloat16)

    outputs = lax.map(one_block, jnp.arange(NBLOCKS, dtype=jnp.int32))
    return outputs.reshape(TOKENS, WIDTH)
```

```python
import functools

import jax
import jax.numpy as jnp
from jax import lax
from jax.experimental import pallas as pl
from jax.experimental.pallas import tpu as pltpu
from jax.sharding import PartitionSpec as P

HEADS = 24
HEAD_DIM = 128
BLOCK = 128
GLOBALS = 2
RANDOMS = 3
LOCAL_HEADS = 3
GROUPS = HEADS // LOCAL_HEADS
MESH = pl.DeviceIdType.MESH
NEG = -1e30


def kernel(ranks, rand_ref, glob_ref, q_hbm, k_hbm, v_hbm, out_hbm, *scratch):
    qs, ks, vs, os = (scratch[3 * i : 3 * i + 3] for i in range(4))
    (send_sem, recv_sem, fwd_send, fwd_recv, own_sem, out_send, out_recv, out_own) = scratch[12:]
    rollout = lax.axis_index("groups")
    me = lax.axis_index("seq")
    group, rank = lax.div(me, ranks), lax.rem(me, ranks)
    blocks = ranks * GROUPS

    def peer(j):
        return lax.rem(group + j, GROUPS)

    def sibling(i):
        return group * ranks + lax.rem(rank + i, ranks)

    def device(index):
        return (rollout, index)

    barrier = pltpu.get_barrier_semaphore()

    @pl.loop(1, GROUPS)
    def _(j):
        pl.semaphore_signal(barrier, inc=1, device_id=device(peer(j) * ranks + rank), device_id_type=MESH)

    @pl.loop(1, ranks)
    def _(i):
        pl.semaphore_signal(barrier, inc=1, device_id=device(sibling(i)), device_id_type=MESH)

    pl.semaphore_wait(barrier, GROUPS - 1 + ranks - 1)

    sources = (q_hbm, k_hbm, v_hbm)

    def columns(owner, h):
        start = pl.multiple_of((owner * LOCAL_HEADS + h) * HEAD_DIM, HEAD_DIM)
        return pl.ds(start, HEAD_DIM)

    def slab(t, h, owner_group):
        if t == 0:
            return qs[h].at[owner_group]
        return (ks, vs)[t - 1][h].at[owner_group * ranks + rank]

    def send(t, h, j):
        return pltpu.make_async_remote_copy(
            src_ref=sources[t].at[:, columns(peer(j), h)],
            dst_ref=slab(t, h, group),
            send_sem=send_sem.at[h, t, j],
            recv_sem=recv_sem.at[h, t, j],
            device_id=device(peer(j) * ranks + rank),
            device_id_type=MESH,
        )

    def received(t, h, j):
        here = slab(t, h, lax.rem(group + GROUPS - j, GROUPS))
        return pltpu.make_async_remote_copy(
            src_ref=here,
            dst_ref=here,
            send_sem=send_sem.at[h, t, j],
            recv_sem=recv_sem.at[h, t, j],
            device_id=device(peer(j) * ranks + rank),
            device_id_type=MESH,
        )

    def own(t, h):
        return pltpu.make_async_copy(
            sources[t].at[:, columns(group, h)], slab(t, h, group), own_sem.at[h, t]
        )

    def forward(t, h, j, i):
        here = slab(t, h, lax.rem(group + GROUPS - j, GROUPS))
        return pltpu.make_async_remote_copy(
            src_ref=here,
            dst_ref=here,
            send_sem=fwd_send.at[h, t - 1, i, j],
            recv_sem=fwd_recv.at[h, t - 1, i, j],
            device_id=device(sibling(i)),
            device_id_type=MESH,
        )

    def forwarded(t, h, j, i):
        block = lax.rem(group + GROUPS - j, GROUPS) * ranks + lax.rem(rank + ranks - i, ranks)
        here = (ks, vs)[t - 1][h].at[block]
        return pltpu.make_async_remote_copy(
            src_ref=here,
            dst_ref=here,
            send_sem=fwd_send.at[h, t - 1, i, j],
            recv_sem=fwd_recv.at[h, t - 1, i, j],
            device_id=device(sibling(i)),
            device_id_type=MESH,
        )

    def send_out(h, j):
        return pltpu.make_async_remote_copy(
            src_ref=os[h].at[peer(j)],
            dst_ref=out_hbm.at[:, columns(group, h)],
            send_sem=out_send.at[h, j],
            recv_sem=out_recv.at[h, j],
            device_id=device(peer(j) * ranks + rank),
            device_id_type=MESH,
        )

    def out_received(h, j):
        owner = lax.rem(group + GROUPS - j, GROUPS)
        return pltpu.make_async_remote_copy(
            src_ref=os[h].at[peer(j)],
            dst_ref=out_hbm.at[:, columns(owner, h)],
            send_sem=out_send.at[h, j],
            recv_sem=out_recv.at[h, j],
            device_id=device(peer(j) * ranks + rank),
            device_id_type=MESH,
        )

    def out_local(h):
        return pltpu.make_async_copy(os[h].at[group], out_hbm.at[:, columns(group, h)], out_own.at[h])

    for h in range(LOCAL_HEADS):
        for t in (1, 2, 0):
            own(t, h).start()

        @pl.loop(1, GROUPS)
        def _(j):
            for t in (1, 2, 0):
                send(t, h, j).start()

    def attend(h, slot):
        block = slot * ranks + rank
        g0, g1 = glob_ref[0], glob_ref[1]

        def bias(b, inside):
            ok = inside & (b != g0) & (b != g1)
            return jnp.where(ok, jnp.float32(0.0), jnp.float32(NEG))

        ids = [
            jnp.maximum(block - 1, 0),
            block,
            jnp.minimum(block + 1, blocks - 1),
            g0,
            g1,
        ] + [rand_ref[block, r] for r in range(RANDOMS)]
        biases = [
            bias(block - 1, block >= 1),
            bias(block, block >= 0),
            bias(block + 1, block + 1 < blocks),
        ]
        query = qs[h][slot]
        key = jnp.concatenate([ks[h][i] for i in ids], axis=0)
        value = jnp.concatenate([vs[h][i] for i in ids], axis=0)
        scores = lax.dot_general(
            query, key, (((1,), (1,)), ((), ())), preferred_element_type=jnp.float32
        ) * (HEAD_DIM ** -0.5)
        parts = [scores[:, n * BLOCK : (n + 1) * BLOCK] for n in range(len(ids))]
        parts = [part + biases[n] if n < 3 else part for n, part in enumerate(parts)]
        top = jnp.max(functools.reduce(jnp.maximum, parts), axis=1, keepdims=True)
        powers = [jnp.exp(part - top) for part in parts]
        total = jnp.sum(functools.reduce(jnp.add, powers), axis=1, keepdims=True)
        inverse = 1.0 / total
        probs = jnp.concatenate([(power * inverse).astype(jnp.bfloat16) for power in powers], axis=1)
        result = lax.dot_general(
            probs, value, (((1,), (0,)), ((), ())), preferred_element_type=jnp.float32
        )
        os[h][slot] = result.astype(jnp.bfloat16)

    for h in range(LOCAL_HEADS):
        for t in (1, 2):
            own(t, h).wait()

            @pl.loop(1, ranks)
            def _(i):
                forward(t, h, 0, i).start()

        @pl.loop(1, GROUPS)
        def _(j):
            for t in (1, 2):
                received(t, h, j).wait_recv()

                @pl.loop(1, ranks)
                def _(i):
                    forward(t, h, j, i).start()

        own(0, h).wait()

        @pl.loop(1, GROUPS)
        def _(j):
            received(0, h, j).wait_recv()

        @pl.loop(1, ranks)
        def _(i):
            @pl.loop(0, GROUPS)
            def _(j):
                for t in (1, 2):
                    forwarded(t, h, j, i).wait_recv()

        @pl.loop(1, GROUPS)
        def _(j):
            attend(h, peer(j))
            send_out(h, j).start()

        attend(h, group)
        out_local(h).start()

    for h in range(LOCAL_HEADS):
        out_local(h).wait()

        @pl.loop(1, GROUPS)
        def _(j):
            for t in range(3):
                send(t, h, j).wait_send()
            send_out(h, j).wait_send()
            out_received(h, j).wait_recv()

        @pl.loop(1, ranks)
        def _(i):
            @pl.loop(0, GROUPS)
            def _(j):
                for t in (1, 2):
                    forward(t, h, j, i).wait_send()


def local(queries, keys, values, rand_blocks, global_ids):
    seq = lax.axis_size("seq")
    ranks = seq // GROUPS
    blocks = rand_blocks.shape[0]
    assert queries.shape[0] == BLOCK and blocks == seq and seq % GROUPS == 0
    tile = (BLOCK, HEAD_DIM)
    anywhere = pl.BlockSpec(memory_space=pl.ANY)
    scalars = pl.BlockSpec(memory_space=pltpu.SMEM)
    dma = pltpu.SemaphoreType.DMA
    return pl.pallas_call(
        functools.partial(kernel, ranks),
        out_shape=jax.ShapeDtypeStruct(queries.shape, jnp.bfloat16),
        in_specs=[scalars, scalars, anywhere, anywhere, anywhere],
        out_specs=anywhere,
        scratch_shapes=[pltpu.VMEM((GROUPS,) + tile, jnp.bfloat16)] * LOCAL_HEADS
        + [pltpu.VMEM((blocks,) + tile, jnp.bfloat16)] * (2 * LOCAL_HEADS)
        + [pltpu.VMEM((GROUPS,) + tile, jnp.bfloat16)] * LOCAL_HEADS
        + [
            dma((LOCAL_HEADS, 3, GROUPS)),
            dma((LOCAL_HEADS, 3, GROUPS)),
            dma((LOCAL_HEADS, 2, ranks, GROUPS)),
            dma((LOCAL_HEADS, 2, ranks, GROUPS)),
            dma((LOCAL_HEADS, 3)),
            dma((LOCAL_HEADS, GROUPS)),
            dma((LOCAL_HEADS, GROUPS)),
            dma((LOCAL_HEADS,)),
        ],
        compiler_params=pltpu.CompilerParams(
            collective_id=0, has_side_effects=True, vmem_limit_bytes=48 << 20
        ),
    )(rand_blocks, global_ids, queries, keys, values)


def solution(mesh):
    placed = (
        P(("groups", "seq"), None),
        P(("groups", "seq"), None),
        P(("groups", "seq"), None),
        P("groups", None),
        P("groups"),
    )
    return jax.shard_map(
        local, mesh=mesh, in_specs=placed, out_specs=P(("groups", "seq"), None), check_vma=False
    )
```

```python
import functools

import jax
import jax.numpy as jnp
from jax import lax
from jax.experimental import pallas as pl
from jax.experimental.pallas import tpu as pltpu
from jax.sharding import PartitionSpec as P

HEADS = 24
HEAD_DIM = 128
BLOCK = 128
GLOBALS = 2
RANDOMS = 3
LOCAL_HEADS = 3
GROUPS = HEADS // LOCAL_HEADS
MESH = pl.DeviceIdType.MESH
NEG = -1e30


def kernel(ranks, rand_ref, glob_ref, q_hbm, k_hbm, v_hbm, out_hbm, *scratch):
    qs, ks, vs, os = (scratch[3 * i : 3 * i + 3] for i in range(4))
    (send_sem, recv_sem, fwd_send, fwd_recv, own_sem, out_send, out_recv, out_own) = scratch[12:]
    rollout = lax.axis_index("groups")
    me = lax.axis_index("seq")
    group, rank = lax.div(me, ranks), lax.rem(me, ranks)
    blocks = ranks * GROUPS

    def peer(j):
        return lax.rem(group + j, GROUPS)

    def sibling(i):
        return group * ranks + lax.rem(rank + i, ranks)

    def device(index):
        return (rollout, index)

    barrier = pltpu.get_barrier_semaphore()

    @pl.loop(1, GROUPS)
    def _(j):
        pl.semaphore_signal(barrier, inc=1, device_id=device(peer(j) * ranks + rank), device_id_type=MESH)

    @pl.loop(1, ranks)
    def _(i):
        pl.semaphore_signal(barrier, inc=1, device_id=device(sibling(i)), device_id_type=MESH)

    pl.semaphore_wait(barrier, GROUPS - 1 + ranks - 1)

    sources = (q_hbm, k_hbm, v_hbm)

    def columns(owner, h):
        start = pl.multiple_of((owner * LOCAL_HEADS + h) * HEAD_DIM, HEAD_DIM)
        return pl.ds(start, HEAD_DIM)

    def slab(t, h, owner_group):
        if t == 0:
            return qs[h].at[owner_group]
        return (ks, vs)[t - 1][h].at[owner_group * ranks + rank]

    def send(t, h, j):
        return pltpu.make_async_remote_copy(
            src_ref=sources[t].at[:, columns(peer(j), h)],
            dst_ref=slab(t, h, group),
            send_sem=send_sem.at[h, t, j],
            recv_sem=recv_sem.at[h, t, j],
            device_id=device(peer(j) * ranks + rank),
            device_id_type=MESH,
        )

    def received(t, h, j):
        here = slab(t, h, lax.rem(group + GROUPS - j, GROUPS))
        return pltpu.make_async_remote_copy(
            src_ref=here,
            dst_ref=here,
            send_sem=send_sem.at[h, t, j],
            recv_sem=recv_sem.at[h, t, j],
            device_id=device(peer(j) * ranks + rank),
            device_id_type=MESH,
        )

    def own(t, h):
        return pltpu.make_async_copy(
            sources[t].at[:, columns(group, h)], slab(t, h, group), own_sem.at[h, t]
        )

    def forward(t, h, j, i):
        here = slab(t, h, lax.rem(group + GROUPS - j, GROUPS))
        return pltpu.make_async_remote_copy(
            src_ref=here,
            dst_ref=here,
            send_sem=fwd_send.at[h, t - 1, i, j],
            recv_sem=fwd_recv.at[h, t - 1, i, j],
            device_id=device(sibling(i)),
            device_id_type=MESH,
        )

    def forwarded(t, h, j, i):
        block = lax.rem(group + GROUPS - j, GROUPS) * ranks + lax.rem(rank + ranks - i, ranks)
        here = (ks, vs)[t - 1][h].at[block]
        return pltpu.make_async_remote_copy(
            src_ref=here,
            dst_ref=here,
            send_sem=fwd_send.at[h, t - 1, i, j],
            recv_sem=fwd_recv.at[h, t - 1, i, j],
            device_id=device(sibling(i)),
            device_id_type=MESH,
        )

    def send_out(h, j):
        return pltpu.make_async_remote_copy(
            src_ref=os[h].at[peer(j)],
            dst_ref=out_hbm.at[:, columns(group, h)],
            send_sem=out_send.at[h, j],
            recv_sem=out_recv.at[h, j],
            device_id=device(peer(j) * ranks + rank),
            device_id_type=MESH,
        )

    def out_received(h, j):
        owner = lax.rem(group + GROUPS - j, GROUPS)
        return pltpu.make_async_remote_copy(
            src_ref=os[h].at[peer(j)],
            dst_ref=out_hbm.at[:, columns(owner, h)],
            send_sem=out_send.at[h, j],
            recv_sem=out_recv.at[h, j],
            device_id=device(peer(j) * ranks + rank),
            device_id_type=MESH,
        )

    def out_local(h):
        return pltpu.make_async_copy(os[h].at[group], out_hbm.at[:, columns(group, h)], out_own.at[h])

    for h in range(LOCAL_HEADS):
        for t in (1, 2, 0):
            own(t, h).start()

        @pl.loop(1, GROUPS)
        def _(j):
            for t in (1, 2, 0):
                send(t, h, j).start()

    def attend(h, slot):
        block = slot * ranks + rank
        g0, g1 = glob_ref[0], glob_ref[1]

        def bias(b, inside):
            ok = inside & (b != g0) & (b != g1)
            return jnp.where(ok, jnp.float32(0.0), jnp.float32(NEG))

        ids = [
            jnp.maximum(block - 1, 0),
            block,
            jnp.minimum(block + 1, blocks - 1),
            g0,
            g1,
        ] + [rand_ref[r, block] for r in range(RANDOMS)]
        biases = [
            bias(block - 1, block >= 1),
            bias(block, block >= 0),
            bias(block + 1, block + 1 < blocks),
        ]
        query = qs[h][slot]
        key = jnp.concatenate([ks[h][i] for i in ids], axis=0)
        value = jnp.concatenate([vs[h][i] for i in ids], axis=0)
        scores = lax.dot_general(
            query, key, (((1,), (1,)), ((), ())), preferred_element_type=jnp.float32
        ) * (HEAD_DIM ** -0.5)
        parts = [scores[:, n * BLOCK : (n + 1) * BLOCK] for n in range(len(ids))]
        parts = [part + biases[n] if n < 3 else part for n, part in enumerate(parts)]
        top = jnp.max(functools.reduce(jnp.maximum, parts), axis=1, keepdims=True)
        powers = [jnp.exp(part - top) for part in parts]
        total = jnp.sum(functools.reduce(jnp.add, powers), axis=1, keepdims=True)
        inverse = 1.0 / total
        probs = jnp.concatenate([(power * inverse).astype(jnp.bfloat16) for power in powers], axis=1)
        result = lax.dot_general(
            probs, value, (((1,), (0,)), ((), ())), preferred_element_type=jnp.float32
        )
        os[h][slot] = result.astype(jnp.bfloat16)

    for h in range(LOCAL_HEADS):
        for t in (1, 2):
            own(t, h).wait()

            @pl.loop(1, ranks)
            def _(i):
                forward(t, h, 0, i).start()

        @pl.loop(1, GROUPS)
        def _(j):
            for t in (1, 2):
                received(t, h, j).wait_recv()

                @pl.loop(1, ranks)
                def _(i):
                    forward(t, h, j, i).start()

        own(0, h).wait()

        @pl.loop(1, GROUPS)
        def _(j):
            received(0, h, j).wait_recv()

        @pl.loop(1, ranks)
        def _(i):
            @pl.loop(0, GROUPS)
            def _(j):
                for t in (1, 2):
                    forwarded(t, h, j, i).wait_recv()

        @pl.loop(1, GROUPS)
        def _(j):
            attend(h, peer(j))
            send_out(h, j).start()

        attend(h, group)
        out_local(h).start()

    for h in range(LOCAL_HEADS):
        out_local(h).wait()

        @pl.loop(1, GROUPS)
        def _(j):
            for t in range(3):
                send(t, h, j).wait_send()
            send_out(h, j).wait_send()
            out_received(h, j).wait_recv()

        @pl.loop(1, ranks)
        def _(i):
            @pl.loop(0, GROUPS)
            def _(j):
                for t in (1, 2):
                    forward(t, h, j, i).wait_send()


def local(queries, keys, values, rand_blocks, global_ids):
    seq = lax.axis_size("seq")
    ranks = seq // GROUPS
    blocks = rand_blocks.shape[0]
    assert queries.shape[0] == BLOCK and blocks == seq and seq % GROUPS == 0
    tile = (BLOCK, HEAD_DIM)
    operands = [
        pltpu.with_memory_space_constraint(x, pltpu.MemorySpace.HBM)
        for x in (rand_blocks.T, global_ids, queries, keys, values)
    ]
    anywhere = pl.BlockSpec(memory_space=pl.ANY)
    scalars = pl.BlockSpec(memory_space=pltpu.SMEM)
    dma = pltpu.SemaphoreType.DMA
    return pl.pallas_call(
        functools.partial(kernel, ranks),
        out_shape=jax.ShapeDtypeStruct(queries.shape, jnp.bfloat16),
        in_specs=[scalars, scalars, anywhere, anywhere, anywhere],
        out_specs=anywhere,
        scratch_shapes=[pltpu.VMEM((GROUPS,) + tile, jnp.bfloat16)] * LOCAL_HEADS
        + [pltpu.VMEM((blocks,) + tile, jnp.bfloat16)] * (2 * LOCAL_HEADS)
        + [pltpu.VMEM((GROUPS,) + tile, jnp.bfloat16)] * LOCAL_HEADS
        + [
            dma((LOCAL_HEADS, 3, GROUPS)),
            dma((LOCAL_HEADS, 3, GROUPS)),
            dma((LOCAL_HEADS, 2, ranks, GROUPS)),
            dma((LOCAL_HEADS, 2, ranks, GROUPS)),
            dma((LOCAL_HEADS, 3)),
            dma((LOCAL_HEADS, GROUPS)),
            dma((LOCAL_HEADS, GROUPS)),
            dma((LOCAL_HEADS,)),
        ],
        compiler_params=pltpu.CompilerParams(
            collective_id=0, has_side_effects=True, vmem_limit_bytes=40 << 20
        ),
    )(*operands)


def solution(mesh):
    placed = (
        P(("groups", "seq"), None),
        P(("groups", "seq"), None),
        P(("groups", "seq"), None),
        P("groups", None),
        P("groups"),
    )
    return jax.shard_map(
        local, mesh=mesh, in_specs=placed, out_specs=P(("groups", "seq"), None), check_vma=False
    )
```

```python
import functools

import jax
import jax.numpy as jnp
from jax import lax
from jax.experimental import pallas as pl
from jax.experimental.pallas import tpu as pltpu
from jax.sharding import PartitionSpec as P

HEADS = 24
HEAD_DIM = 128
BLOCK = 128
GLOBALS = 2
RANDOMS = 3
LOCAL_HEADS = 3
GROUPS = HEADS // LOCAL_HEADS
MESH = pl.DeviceIdType.MESH
NEG = -1e30


def kernel(ranks, rand_ref, glob_ref, q_hbm, k_hbm, v_hbm, out_hbm, *scratch):
    qs, ks, vs, os = (scratch[3 * i : 3 * i + 3] for i in range(4))
    (send_sem, recv_sem, fwd_send, fwd_recv, own_sem, out_send, out_recv, out_own, late_sem) = scratch[12:]
    rollout = lax.axis_index("groups")
    me = lax.axis_index("seq")
    group, rank = lax.div(me, ranks), lax.rem(me, ranks)
    blocks = ranks * GROUPS

    def for_peers(body):
        @pl.loop(1, GROUPS)
        def _(j):
            body(lax.rem(group + j, GROUPS))

    def sibling(i):
        return group * ranks + lax.rem(rank + i, ranks)

    def device(index):
        return (rollout, index)

    barrier = pltpu.get_barrier_semaphore()

    late_from = GROUPS - GROUPS // 4
    late = group >= late_from

    @for_peers
    def _(p):
        @pl.when(jnp.logical_not(late) | (p >= late_from))
        def _():
            pl.semaphore_signal(barrier, inc=1, device_id=device(p * ranks + rank), device_id_type=MESH)

    @pl.loop(1, ranks)
    def _(i):
        pl.semaphore_signal(barrier, inc=1, device_id=device(sibling(i)), device_id_type=MESH)

    pl.semaphore_wait(barrier, jnp.where(late, GROUPS, late_from) - 1 + ranks - 1)

    @pl.when(late)
    def _():
        @pl.loop(0, late_from)
        def _(p):
            pl.semaphore_signal(late_sem, inc=1, device_id=device(p * ranks + rank), device_id_type=MESH)

    sources = (q_hbm, k_hbm, v_hbm)

    def columns(owner, h):
        start = pl.multiple_of((owner * LOCAL_HEADS + h) * HEAD_DIM, HEAD_DIM)
        return pl.ds(start, HEAD_DIM)

    def slab(t, h, owner_group):
        if t == 0:
            return qs[h].at[owner_group]
        return (ks, vs)[t - 1][h].at[owner_group * ranks + rank]

    def send(t, h, p):
        return pltpu.make_async_remote_copy(
            src_ref=sources[t].at[:, columns(p, h)],
            dst_ref=slab(t, h, group),
            send_sem=send_sem.at[h, t, p],
            recv_sem=recv_sem.at[h, t, group],
            device_id=device(p * ranks + rank),
            device_id_type=MESH,
        )

    def received(t, h, p):
        here = slab(t, h, p)
        return pltpu.make_async_remote_copy(
            src_ref=here,
            dst_ref=here,
            send_sem=send_sem.at[h, t, p],
            recv_sem=recv_sem.at[h, t, p],
            device_id=device(p * ranks + rank),
            device_id_type=MESH,
        )

    def own(t, h):
        return pltpu.make_async_copy(
            sources[t].at[:, columns(group, h)], slab(t, h, group), own_sem.at[h, t]
        )

    def forward(t, h, p, i):
        here = slab(t, h, p)
        return pltpu.make_async_remote_copy(
            src_ref=here,
            dst_ref=here,
            send_sem=fwd_send.at[h, t - 1, i, p],
            recv_sem=fwd_recv.at[h, t - 1, i, p],
            device_id=device(sibling(i)),
            device_id_type=MESH,
        )

    def forwarded(t, h, p, i):
        here = (ks, vs)[t - 1][h].at[p * ranks + lax.rem(rank + ranks - i, ranks)]
        return pltpu.make_async_remote_copy(
            src_ref=here,
            dst_ref=here,
            send_sem=fwd_send.at[h, t - 1, i, p],
            recv_sem=fwd_recv.at[h, t - 1, i, p],
            device_id=device(sibling(i)),
            device_id_type=MESH,
        )

    def send_out(h, p):
        return pltpu.make_async_remote_copy(
            src_ref=os[h].at[p],
            dst_ref=out_hbm.at[:, columns(group, h)],
            send_sem=out_send.at[h, p],
            recv_sem=out_recv.at[h, group],
            device_id=device(p * ranks + rank),
            device_id_type=MESH,
        )

    def out_received(h, p):
        return pltpu.make_async_remote_copy(
            src_ref=os[h].at[p],
            dst_ref=out_hbm.at[:, columns(p, h)],
            send_sem=out_send.at[h, p],
            recv_sem=out_recv.at[h, p],
            device_id=device(p * ranks + rank),
            device_id_type=MESH,
        )

    def out_local(h):
        return pltpu.make_async_copy(os[h].at[group], out_hbm.at[:, columns(group, h)], out_own.at[h])

    for h in range(LOCAL_HEADS):
        @for_peers
        def _(p):
            @pl.when(late | (p < late_from) | (h > 0))
            def _():
                for t in (1, 2, 0):
                    send(t, h, p).start()

        if h == 0:
            @pl.when(jnp.logical_not(late))
            def _():
                pl.semaphore_wait(late_sem, GROUPS - late_from)

                @pl.loop(late_from, GROUPS)
                def _(p):
                    for t in (1, 2, 0):
                        send(t, h, p).start()

        for t in (1, 2, 0):
            own(t, h).start()

    def attend(h, slot):
        block = slot * ranks + rank
        g0, g1 = glob_ref[0], glob_ref[1]

        def bias(b, inside):
            ok = inside & (b != g0) & (b != g1)
            return jnp.where(ok, jnp.float32(0.0), jnp.float32(NEG))

        ids = [
            jnp.maximum(block - 1, 0),
            block,
            jnp.minimum(block + 1, blocks - 1),
            g0,
            g1,
        ] + [rand_ref[r, block] for r in range(RANDOMS)]
        biases = [
            bias(block - 1, block >= 1),
            bias(block, block >= 0),
            bias(block + 1, block + 1 < blocks),
        ]
        query = qs[h][slot]
        key = jnp.concatenate([ks[h][i] for i in ids], axis=0)
        value = jnp.concatenate([vs[h][i] for i in ids], axis=0)
        scores = lax.dot_general(
            query, key, (((1,), (1,)), ((), ())), preferred_element_type=jnp.float32
        ) * (HEAD_DIM ** -0.5)
        parts = [scores[:, n * BLOCK : (n + 1) * BLOCK] for n in range(len(ids))]
        parts = [part + biases[n] if n < 3 else part for n, part in enumerate(parts)]
        top = jnp.max(functools.reduce(jnp.maximum, parts), axis=1, keepdims=True)
        powers = [jnp.exp(part - top) for part in parts]
        total = jnp.sum(functools.reduce(jnp.add, powers), axis=1, keepdims=True)
        inverse = 1.0 / total
        probs = jnp.concatenate([(power * inverse).astype(jnp.bfloat16) for power in powers], axis=1)
        result = lax.dot_general(
            probs, value, (((1,), (0,)), ((), ())), preferred_element_type=jnp.float32
        )
        os[h][slot] = result.astype(jnp.bfloat16)

    for h in range(LOCAL_HEADS):
        for t in (1, 2):
            own(t, h).wait()

            @pl.loop(1, ranks)
            def _(i):
                forward(t, h, group, i).start()

        @for_peers
        def _(p):
            for t in (1, 2):
                received(t, h, p).wait_recv()

                @pl.loop(1, ranks)
                def _(i):
                    forward(t, h, p, i).start()

        own(0, h).wait()

        @for_peers
        def _(p):
            received(0, h, p).wait_recv()

        @pl.loop(1, ranks)
        def _(i):
            @pl.loop(0, GROUPS)
            def _(p):
                for t in (1, 2):
                    forwarded(t, h, p, i).wait_recv()

        @pl.loop(0, GROUPS)
        def _(p):
            attend(h, p)

            @pl.when(p != group)
            def _():
                send_out(h, p).start()

        out_local(h).start()

    for h in range(LOCAL_HEADS):
        out_local(h).wait()

        @for_peers
        def _(p):
            for t in range(3):
                send(t, h, p).wait_send()
            send_out(h, p).wait_send()
            out_received(h, p).wait_recv()

        @pl.loop(1, ranks)
        def _(i):
            @pl.loop(0, GROUPS)
            def _(p):
                for t in (1, 2):
                    forward(t, h, p, i).wait_send()


def local(queries, keys, values, rand_blocks, global_ids):
    seq = lax.axis_size("seq")
    ranks = seq // GROUPS
    blocks = rand_blocks.shape[0]
    assert queries.shape[0] == BLOCK and blocks == seq and seq % GROUPS == 0
    tile = (BLOCK, HEAD_DIM)
    sources = [pltpu.with_memory_space_constraint(x, pltpu.MemorySpace.HBM) for x in (rand_blocks.T, global_ids, queries, keys, values)]
    anywhere = pl.BlockSpec(memory_space=pl.ANY)
    scalars = pl.BlockSpec(memory_space=pltpu.SMEM)
    dma = pltpu.SemaphoreType.DMA
    return pl.pallas_call(
        functools.partial(kernel, ranks),
        out_shape=jax.ShapeDtypeStruct(queries.shape, jnp.bfloat16),
        in_specs=[scalars, scalars, anywhere, anywhere, anywhere],
        out_specs=anywhere,
        scratch_shapes=[pltpu.VMEM((GROUPS,) + tile, jnp.bfloat16)] * LOCAL_HEADS
        + [pltpu.VMEM((blocks,) + tile, jnp.bfloat16)] * (2 * LOCAL_HEADS)
        + [pltpu.VMEM((GROUPS,) + tile, jnp.bfloat16)] * LOCAL_HEADS
        + [
            dma((LOCAL_HEADS, 3, GROUPS)),
            dma((LOCAL_HEADS, 3, GROUPS)),
            dma((LOCAL_HEADS, 2, ranks, GROUPS)),
            dma((LOCAL_HEADS, 2, ranks, GROUPS)),
            dma((LOCAL_HEADS, 3)),
            dma((LOCAL_HEADS, GROUPS)),
            dma((LOCAL_HEADS, GROUPS)),
            dma((LOCAL_HEADS,)),
            pltpu.SemaphoreType.REGULAR,
        ],
        compiler_params=pltpu.CompilerParams(
            collective_id=0, has_side_effects=True, vmem_limit_bytes=40 << 20
        ),
    )(*sources)


def solution(mesh):
    placed = (
        P(("groups", "seq"), None),
        P(("groups", "seq"), None),
        P(("groups", "seq"), None),
        P("groups", None),
        P("groups"),
    )
    return jax.shard_map(
        local, mesh=mesh, in_specs=placed, out_specs=P(("groups", "seq"), None), check_vma=False
    )
```

```python
import functools

import jax
import jax.numpy as jnp
from jax import lax
from jax.experimental import pallas as pl
from jax.experimental.pallas import tpu as pltpu
from jax.sharding import PartitionSpec as P

HEADS = 24
HEAD_DIM = 128
BLOCK = 128
GLOBALS = 2
RANDOMS = 3
LOCAL_HEADS = 3
GROUPS = HEADS // LOCAL_HEADS
MESH = pl.DeviceIdType.MESH
NEG = -1e30


def kernel(ranks, rand_ref, glob_ref, q_hbm, k_hbm, v_hbm, out_hbm, *scratch):
    qs, ks, vs, os = (scratch[3 * i : 3 * i + 3] for i in range(4))
    (send_sem, recv_sem, fwd_send, fwd_recv, own_sem, out_send, out_recv, out_own, late_sem) = scratch[12:]
    rollout = lax.axis_index("groups")
    me = lax.axis_index("seq")
    group, rank = lax.div(me, ranks), lax.rem(me, ranks)
    blocks = ranks * GROUPS

    def for_peers(body):
        @pl.loop(0, GROUPS - 1)
        def _(j):
            body(j + jnp.where(j >= group, 1, 0))

    def sibling(i):
        return group * ranks + lax.rem(rank + i, ranks)

    def device(index):
        return (rollout, index)

    barrier = pltpu.get_barrier_semaphore()

    late_from = GROUPS - GROUPS // 4
    late = group >= late_from

    @for_peers
    def _(p):
        @pl.when(jnp.logical_not(late) | (p >= late_from))
        def _():
            pl.semaphore_signal(barrier, inc=1, device_id=device(p * ranks + rank), device_id_type=MESH)

    @pl.loop(1, ranks)
    def _(i):
        pl.semaphore_signal(barrier, inc=1, device_id=device(sibling(i)), device_id_type=MESH)

    pl.semaphore_wait(barrier, jnp.where(late, GROUPS, late_from) - 1 + ranks - 1)

    @pl.when(late)
    def _():
        @pl.loop(0, late_from)
        def _(p):
            pl.semaphore_signal(late_sem, inc=1, device_id=device(p * ranks + rank), device_id_type=MESH)

    sources = (q_hbm, k_hbm, v_hbm)

    def columns(owner, h):
        start = pl.multiple_of((owner * LOCAL_HEADS + h) * HEAD_DIM, HEAD_DIM)
        return pl.ds(start, HEAD_DIM)

    def slab(t, h, owner_group):
        if t == 0:
            return qs[h].at[owner_group]
        return (ks, vs)[t - 1][h].at[owner_group * ranks + rank]

    def send(t, h, p):
        return pltpu.make_async_remote_copy(
            src_ref=sources[t].at[:, columns(p, h)],
            dst_ref=slab(t, h, group),
            send_sem=send_sem.at[h, t, p],
            recv_sem=recv_sem.at[h, t, group],
            device_id=device(p * ranks + rank),
            device_id_type=MESH,
        )

    def received(t, h, p):
        here = slab(t, h, p)
        return pltpu.make_async_remote_copy(
            src_ref=here,
            dst_ref=here,
            send_sem=send_sem.at[h, t, p],
            recv_sem=recv_sem.at[h, t, p],
            device_id=device(p * ranks + rank),
            device_id_type=MESH,
        )

    def own(t, h):
        return pltpu.make_async_copy(
            sources[t].at[:, columns(group, h)], slab(t, h, group), own_sem.at[h, t]
        )

    def forward(t, h, p, i):
        here = slab(t, h, p)
        return pltpu.make_async_remote_copy(
            src_ref=here,
            dst_ref=here,
            send_sem=fwd_send.at[h, t - 1, i, p],
            recv_sem=fwd_recv.at[h, t - 1, i, p],
            device_id=device(sibling(i)),
            device_id_type=MESH,
        )

    def forwarded(t, h, p, i):
        here = (ks, vs)[t - 1][h].at[p * ranks + lax.rem(rank + ranks - i, ranks)]
        return pltpu.make_async_remote_copy(
            src_ref=here,
            dst_ref=here,
            send_sem=fwd_send.at[h, t - 1, i, p],
            recv_sem=fwd_recv.at[h, t - 1, i, p],
            device_id=device(sibling(i)),
            device_id_type=MESH,
        )

    def send_out(h, p):
        return pltpu.make_async_remote_copy(
            src_ref=os[h].at[p],
            dst_ref=out_hbm.at[:, columns(group, h)],
            send_sem=out_send.at[h, p],
            recv_sem=out_recv.at[h, group],
            device_id=device(p * ranks + rank),
            device_id_type=MESH,
        )

    def out_received(h, p):
        return pltpu.make_async_remote_copy(
            src_ref=os[h].at[p],
            dst_ref=out_hbm.at[:, columns(p, h)],
            send_sem=out_send.at[h, p],
            recv_sem=out_recv.at[h, p],
            device_id=device(p * ranks + rank),
            device_id_type=MESH,
        )

    def out_local(h):
        return pltpu.make_async_copy(os[h].at[group], out_hbm.at[:, columns(group, h)], out_own.at[h])

    for h in range(LOCAL_HEADS):
        @for_peers
        def _(p):
            @pl.when(late | (p < late_from) | (h > 0))
            def _():
                for t in (1, 2, 0):
                    send(t, h, p).start()

        if h == 0:
            @pl.when(jnp.logical_not(late))
            def _():
                pl.semaphore_wait(late_sem, GROUPS - late_from)

                @pl.loop(late_from, GROUPS)
                def _(p):
                    for t in (1, 2, 0):
                        send(t, h, p).start()

        for t in (1, 2, 0):
            own(t, h).start()

    def attend(h, slot):
        block = slot * ranks + rank
        g0, g1 = glob_ref[0], glob_ref[1]

        def bias(b, inside):
            ok = inside & (b != g0) & (b != g1)
            return jnp.where(ok, jnp.float32(0.0), jnp.float32(NEG))

        ids = [
            jnp.maximum(block - 1, 0),
            block,
            jnp.minimum(block + 1, blocks - 1),
            g0,
            g1,
        ] + [rand_ref[r, block] for r in range(RANDOMS)]
        biases = [
            bias(block - 1, block >= 1),
            bias(block, block >= 0),
            bias(block + 1, block + 1 < blocks),
        ]
        query = qs[h][slot]
        key = jnp.concatenate([ks[h][i] for i in ids], axis=0)
        value = jnp.concatenate([vs[h][i] for i in ids], axis=0)
        scores = lax.dot_general(
            query, key, (((1,), (1,)), ((), ())), preferred_element_type=jnp.float32
        ) * (HEAD_DIM ** -0.5)
        parts = [scores[:, n * BLOCK : (n + 1) * BLOCK] for n in range(len(ids))]
        parts = [part + biases[n] if n < 3 else part for n, part in enumerate(parts)]
        top = jnp.max(functools.reduce(jnp.maximum, parts), axis=1, keepdims=True)
        powers = [jnp.exp(part - top) for part in parts]
        total = jnp.sum(functools.reduce(jnp.add, powers), axis=1, keepdims=True)
        inverse = 1.0 / total
        probs = jnp.concatenate([(power * inverse).astype(jnp.bfloat16) for power in powers], axis=1)
        result = lax.dot_general(
            probs, value, (((1,), (0,)), ((), ())), preferred_element_type=jnp.float32
        )
        os[h][slot] = result.astype(jnp.bfloat16)

    for h in range(LOCAL_HEADS):
        for t in (1, 2):
            own(t, h).wait()

            @pl.loop(1, ranks)
            def _(i):
                forward(t, h, group, i).start()

        @for_peers
        def _(p):
            for t in (1, 2):
                received(t, h, p).wait_recv()

                @pl.loop(1, ranks)
                def _(i):
                    forward(t, h, p, i).start()

        own(0, h).wait()

        @for_peers
        def _(p):
            received(0, h, p).wait_recv()

        @pl.loop(1, ranks)
        def _(i):
            @pl.loop(0, GROUPS)
            def _(p):
                for t in (1, 2):
                    forwarded(t, h, p, i).wait_recv()

        @pl.loop(0, GROUPS)
        def _(p):
            attend(h, p)

            @pl.when(p != group)
            def _():
                send_out(h, p).start()

        out_local(h).start()

    for h in range(LOCAL_HEADS):
        out_local(h).wait()

        @for_peers
        def _(p):
            for t in range(3):
                send(t, h, p).wait_send()
            send_out(h, p).wait_send()
            out_received(h, p).wait_recv()

        @pl.loop(1, ranks)
        def _(i):
            @pl.loop(0, GROUPS)
            def _(p):
                for t in (1, 2):
                    forward(t, h, p, i).wait_send()


def local(queries, keys, values, rand_blocks, global_ids):
    seq = lax.axis_size("seq")
    ranks = seq // GROUPS
    blocks = rand_blocks.shape[0]
    assert queries.shape[0] == BLOCK and blocks == seq and seq % GROUPS == 0
    tile = (BLOCK, HEAD_DIM)
    sources = [pltpu.with_memory_space_constraint(x, pltpu.MemorySpace.HBM) for x in (rand_blocks.T, global_ids, queries, keys, values)]
    anywhere = pl.BlockSpec(memory_space=pl.ANY)
    scalars = pl.BlockSpec(memory_space=pltpu.SMEM)
    dma = pltpu.SemaphoreType.DMA
    return pl.pallas_call(
        functools.partial(kernel, ranks),
        out_shape=jax.ShapeDtypeStruct(queries.shape, jnp.bfloat16),
        in_specs=[scalars, scalars, anywhere, anywhere, anywhere],
        out_specs=anywhere,
        scratch_shapes=[pltpu.VMEM((GROUPS,) + tile, jnp.bfloat16)] * LOCAL_HEADS
        + [pltpu.VMEM((blocks,) + tile, jnp.bfloat16)] * (2 * LOCAL_HEADS)
        + [pltpu.VMEM((GROUPS,) + tile, jnp.bfloat16)] * LOCAL_HEADS
        + [
            dma((LOCAL_HEADS, 3, GROUPS)),
            dma((LOCAL_HEADS, 3, GROUPS)),
            dma((LOCAL_HEADS, 2, ranks, GROUPS)),
            dma((LOCAL_HEADS, 2, ranks, GROUPS)),
            dma((LOCAL_HEADS, 3)),
            dma((LOCAL_HEADS, GROUPS)),
            dma((LOCAL_HEADS, GROUPS)),
            dma((LOCAL_HEADS,)),
            pltpu.SemaphoreType.REGULAR,
        ],
        compiler_params=pltpu.CompilerParams(
            collective_id=0, has_side_effects=True, vmem_limit_bytes=40 << 20
        ),
    )(*sources)


def solution(mesh):
    placed = (
        P(("groups", "seq"), None),
        P(("groups", "seq"), None),
        P(("groups", "seq"), None),
        P("groups", None),
        P("groups"),
    )
    return jax.shard_map(
        local, mesh=mesh, in_specs=placed, out_specs=P(("groups", "seq"), None), check_vma=False
    )
```
